512 devices in a mesh: blk: 32 (over y, x), head: 16 (over z, core).
Axes of the slice: x: 4, y: 8, z: 8, core: 2. Of those that a mesh axis runs over, the one named last changes fastest.
Arguments:
- tokens: bfloat16 [2048, 4096], P('blk', 'head'), may hold values from -6 to 6
- queries: bfloat16 [2048, 36864], P('blk', 'head'), may hold values from -600 to 600
- latents: bfloat16 [2048, 576], P('blk'), may hold values from -6 to 6
- value_up: bfloat16 [64, 512, 128], P('head'), may hold values from -0.25 to 0.25
- out_proj: bfloat16 [8192, 4096], P('head', 'blk'), may hold values from -0.09375 to 0.09375
- expert_ids: int32 [2048, 8], P('blk'), may hold values from 0 to 31, all different within a row; in each aligned block of 64 rows (0 to 63, 64 to 127, ...) at most 20 rows name the same one
- expert_gates: float32 [2048, 8], P('blk'), may hold values from 0.05 to 0.5
- w_gate: bfloat16 [32, 4096, 2048], P('blk', None, 'head'), may hold values from -0.09375 to 0.09375
- w_up: bfloat16 [32, 4096, 2048], P('blk', None, 'head'), may hold values from -0.09375 to 0.09375
- w_down: bfloat16 [32, 2048, 4096], P('blk', None, 'head'), may hold values from -0.125 to 0.125
Outputs:
- result: bfloat16 [2048, 4096], P('blk', 'head')
The draws below stay inside these ranges and needn't reach their ends.
Inputs may be any that keep to these rules, and one draw needn't show every extreme that they name: `expert_ids`: among the tokens of one index of blk (aligned blocks of 64 rows) at most 20 choose one expert, and some expert is chosen by exactly 20 of them; the experts of one row differ.
All inputs are finite; a program needn't handle non-finite values.
Results may differ from the reference program's by a relative error of at most 0.013.
Values may be sent and summed in bfloat16 or wider, within the bound.
No kernel may reach another device: no remote copies, remote signals or barrier semaphores. Data moves between devices by JAX's collectives and lax.ppermute only.
A program may use at most 64 MiB of HBM per device.

```python
import math
import jax
import jax.numpy as jnp
import numpy as np
from jax import lax

D = 4096
LAT = 512
ROPE = 64
QKNOPE = 128
VDIM = 128
HEADS = 64
FF = 2048
EXPERTS = 32
TOPK = 8
TOK_DEV = 64
CAP = 20
TOKENS = 2048
N_BLK = 32


def latent_table(key):
    base = jax.random.truncated_normal(jax.random.fold_in(key, 11), -6.0, 6.0, (TOKENS, LAT + ROPE), jnp.float32)
    return base


def draw_latents(key, part):
    return latent_table(key).astype(jnp.bfloat16)


def draw_queries(key, part):
    base = jax.random.truncated_normal(jax.random.fold_in(key, 23), -6.0, 6.0, (TOKENS, HEADS, LAT + ROPE), jnp.float32)
    return base.reshape(TOKENS, HEADS * (LAT + ROPE)).astype(jnp.bfloat16)


def levels(own_key, dims, cuts, low, top_value):
    gain = 1.0
    for dim, shards_of in cuts:
        steps = jax.random.uniform(jax.random.fold_in(jax.random.fold_in(own_key, 6), dim), (shards_of,), jnp.float32, low / len(cuts), top_value / len(cuts))
        gain = gain * jnp.repeat(jnp.exp(steps), dims[dim] // shards_of).reshape((-1,) + (1,) * (len(dims) - 1 - dim))
    return gain


def assign_block(stream_key, own, number, rows, amount, top, limit, lean):
    sequence = jax.random.permutation(stream_key, amount)
    crowded, common = load_shares(amount, rows * top, limit, lean, True), load_shares(amount, rows * top, limit, lean, False)
    places = jnp.arange(amount)

    def named(tallies, offset_by):
        used = int((tallies > 0).sum())
        fixed = max(1, used // 4)
        shifted = fixed + (places - fixed + offset_by * (used - fixed)) % max(1, amount - fixed)
        return jnp.zeros((amount,), jnp.int32).at[sequence[jnp.where(places < fixed, places, shifted)]].set(jnp.asarray(tallies, jnp.int32))

    tallies = jnp.where(number % 4 == 0, named(crowded, number // 4), named(common, number - number // 4 - 1))
    mixed = jax.random.permutation(jax.random.fold_in(own, 3), amount)
    giver, taker = mixed[0:amount // 2 * 2:2], mixed[1:amount // 2 * 2:2]
    margin = jnp.minimum(tallies[giver] - 1, limit - tallies[taker]) // 2
    margin = jnp.where((giver == sequence[0]) | (taker == sequence[0]) | (tallies[taker] == 0), 0, jnp.maximum(margin, 0))
    shifted = jax.random.randint(jax.random.fold_in(own, 4), (amount // 2,), 0, 1 << 20) % (margin + 1)
    tallies = tallies.at[giver].add(-shifted).at[taker].add(shifted)
    labels = jnp.searchsorted(jnp.cumsum(tallies), jnp.arange(rows * top), side="right").astype(jnp.int32)
    listing = labels.reshape(top, rows).T
    listing = listing[jax.random.permutation(jax.random.fold_in(own, 1), rows)]
    offset_by = jax.random.randint(jax.random.fold_in(own, 2), (rows, 1), 0, top)
    return jnp.take_along_axis(listing, (jnp.arange(top)[None, :] + offset_by) % top, axis=1)


def load_shares(number_of, total, reach, skew, full):
    portions = [(1 << 20) // math.isqrt(grade ** skew) + 1 for grade in range(1, number_of + 1)]
    largest = reach if full else min(reach, max(-(-total // number_of), total * portions[0] // sum(portions)))
    least = 1 if total - largest >= number_of - 1 else 0
    holding, rest = [largest] + [least] * (number_of - 1), total - largest - least * (number_of - 1)
    while rest > 0:
        movable = [i for i in range(1, number_of) if holding[i] < largest] or [i for i in range(1, number_of) if holding[i] < reach]
        whole, remaining = sum([portions[i] for i in movable]), rest
        for i in movable:
            more = min(reach - holding[i], max(1, remaining * portions[i] // whole), rest)
            holding[i] = holding[i] + more
            rest = rest - more
    return np.array(holding)


def normal_values(key, shape, deviation, bound, shards=(), held_as=jnp.bfloat16):
    drawn = deviation * jax.random.normal(key, shape, jnp.float32)
    if shards:
        drawn = drawn * levels(key, shape, shards, -0.22, 0.18)
    return jnp.clip(drawn, -bound, bound).astype(held_as)


def setup_inputs(seed: int = 0) -> dict:
    splits = jax.random.split(jax.random.key(seed), 11)
    tokens = normal_values(splits[0], (TOKENS, D), 1.0, 6.0, ((0, 32), (1, 16)))
    queries = draw_queries(jax.random.fold_in(splits[10], 71), 0)
    latents = draw_latents(jax.random.fold_in(splits[10], 71), 0)
    value_up = normal_values(splits[3], (HEADS, LAT, VDIM), LAT ** -0.5, 0.25, ((0, 16),))
    out_proj = normal_values(splits[4], (HEADS * VDIM, D), (HEADS * VDIM // 2) ** -0.5, 0.09375, ((0, 16), (1, 32)))
    expert_ids_keys = jax.random.split(jax.random.fold_in(splits[5], 1), TOKENS // TOK_DEV)
    expert_ids_turns = jax.random.permutation(jax.random.fold_in(splits[5], 3), TOKENS // TOK_DEV)
    expert_ids = jax.vmap(lambda own, number: assign_block(jax.random.fold_in(splits[5], 2), own, number, TOK_DEV, EXPERTS, TOPK, CAP, 2))(expert_ids_keys, expert_ids_turns).reshape((TOKENS, TOPK))
    expert_gates = jnp.clip(0.05 + 0.45 * jax.random.uniform(splits[6], (TOKENS, TOPK), jnp.float32) ** levels(splits[6], (TOKENS, TOPK), ((0, 32),), -0.2, 0.2), 0.05, 0.5)
    w_gate = normal_values(splits[7], (EXPERTS, D, FF), D ** -0.5, 0.09375, ((0, 32), (2, 16)))
    w_up = normal_values(splits[8], (EXPERTS, D, FF), D ** -0.5, 0.09375, ((0, 32), (2, 16)))
    w_down = normal_values(splits[9], (EXPERTS, FF, D), FF ** -0.5, 0.125, ((0, 32), (2, 16)))
    return {"tokens": tokens, "queries": queries, "latents": latents, "value_up": value_up, "out_proj": out_proj, "expert_ids": expert_ids, "expert_gates": expert_gates, "w_gate": w_gate, "w_up": w_up, "w_down": w_down}


def reference(tokens, queries, latents, value_up, out_proj, expert_ids, expert_gates, w_gate, w_up, w_down):
    score_scale = (QKNOPE + ROPE) ** (-0.5)
    key_width = LAT + ROPE
    positions = jnp.arange(TOKENS, dtype=jnp.int32)
    causal = positions[None, :] <= positions[:, None]
    values = latents[:, :LAT]
    query_heads = queries.reshape(TOKENS, HEADS, key_width).transpose(1, 0, 2)

    def one_head(inputs):
        query_one, lift_one = inputs
        scores = jnp.dot(query_one, latents.T, preferred_element_type=jnp.float32) * score_scale
        scores = jnp.where(causal, scores, -jnp.inf)
        row_max = lax.optimization_barrier(jnp.max(scores, axis=1, keepdims=True))
        weights = jnp.where(causal, jnp.exp(scores - row_max), 0.0)
        denominator = lax.optimization_barrier(jnp.sum(weights, axis=1, keepdims=True))
        context = (jnp.dot(weights.astype(jnp.bfloat16), values, preferred_element_type=jnp.float32) / denominator).astype(jnp.bfloat16)
        return jnp.dot(context, lift_one, preferred_element_type=jnp.float32).astype(jnp.bfloat16)
    lifted = lax.map(one_head, (query_heads, value_up))
    lifted = lifted.transpose(1, 0, 2).reshape(TOKENS, HEADS * VDIM)
    attended = jnp.dot(lifted, out_proj, preferred_element_type=jnp.float32)
    mid_state = (tokens.astype(jnp.float32) + attended).astype(jnp.bfloat16)
    mid_wide = mid_state.astype(jnp.float32)
    squares = lax.optimization_barrier(jnp.sum(mid_wide * mid_wide, axis=1))
    normed = (mid_wide * lax.rsqrt(squares / D + 1e-06)[:, None]).astype(jnp.bfloat16)
    most_load = N_BLK * CAP
    flat_ids = expert_ids.reshape(-1)
    flat_gates = expert_gates.reshape(-1)
    flat_tokens = jnp.arange(TOKENS * TOPK, dtype=jnp.int32) // TOPK

    def one_expert(expert):
        chosen = flat_ids == expert
        where_idx = jnp.nonzero(chosen, size=most_load, fill_value=0)[0].astype(jnp.int32)
        live = jnp.arange(most_load, dtype=jnp.int32) < jnp.sum(chosen.astype(jnp.int32))
        rows_in = normed[flat_tokens[where_idx]]
        gate_val = jnp.dot(rows_in, w_gate[expert], preferred_element_type=jnp.float32)
        up_val = jnp.dot(rows_in, w_up[expert], preferred_element_type=jnp.float32)
        activation = (jax.nn.silu(gate_val) * up_val).astype(jnp.bfloat16)
        expert_out = jnp.dot(activation, w_down[expert], preferred_element_type=jnp.float32).astype(jnp.bfloat16)
        weight_row = jnp.where(live, flat_gates[where_idx], 0.0)
        return (where_idx, expert_out.astype(jnp.float32) * weight_row[:, None])
    index_all, contrib = lax.map(one_expert, jnp.arange(EXPERTS, dtype=jnp.int32))
    routed = jnp.zeros((TOKENS * TOPK, D), jnp.float32).at[index_all.reshape(-1)].add(contrib.reshape(-1, D))
    routed = lax.optimization_barrier(jnp.sum(routed.reshape(TOKENS, TOPK, D), axis=1))
    return (mid_wide + routed).astype(jnp.bfloat16)
```

```python
import functools

import jax
import jax.numpy as jnp
from jax import lax
from jax.experimental import pallas as pl
from jax.experimental.pallas import tpu as pltpu
from jax.sharding import PartitionSpec as P

D = 4096
LAT = 512
ROPE = 64
QKNOPE = 128
VDIM = 128
EXPERTS = 32
CAP = 20
SLOTS = EXPERTS * CAP
TOK = 64
HALF = TOK // 2
N_BLK = 32
N_HEAD = 16
N_X = 4
N_Y = 8
HEADS_HERE = 4
KEYS = N_BLK * HALF
SCALE = (QKNOPE + ROPE) ** (-0.5)

X_GROUPS = [[y * N_X + x for x in range(N_X)] for y in range(N_Y)]
Y_GROUPS = [[y * N_X + x for y in range(N_Y)] for x in range(N_X)]
XH_GROUPS = [[y * 64 + i for i in range(64)] for y in range(N_Y)]
CORE_SWAP = [(i, i ^ 1) for i in range(N_HEAD)]


def attention_kernel(place_ref, q_ref, own_ref, other_ref, lift_ref, out_ref):
    width = LAT + ROPE
    q_all = q_ref[...]
    q_rows = jnp.concatenate(
        [q_all[:, h * width : (h + 1) * width] for h in range(HEADS_HERE)], axis=0
    )
    rows = HEADS_HERE * TOK
    first = place_ref[0] * TOK
    core = place_ref[1]
    query_pos = first + (lax.broadcasted_iota(jnp.int32, (rows, KEYS), 0) & (TOK - 1))
    key_idx = lax.broadcasted_iota(jnp.int32, (rows, KEYS), 1)
    key_base = (key_idx >> 5) * TOK + (key_idx & (HALF - 1))
    scores, maxes, masks = [], [], []
    for part, ref in ((core, own_ref), (1 - core, other_ref)):
        raw = lax.dot_general(
            q_rows, ref[...], (((1,), (1,)), ((), ())), preferred_element_type=jnp.float32
        )
        allowed = key_base + part * HALF <= query_pos
        raw = jnp.where(allowed, raw * SCALE, -1e30)
        scores.append(raw)
        masks.append(allowed)
        maxes.append(jnp.max(raw, axis=1, keepdims=True))
    row_max = jnp.maximum(maxes[0], maxes[1])
    denominator = 0.0
    context = 0.0
    for raw, allowed, ref in zip(scores, masks, (own_ref, other_ref)):
        weights = jnp.where(allowed, jnp.exp(raw - row_max), 0.0)
        denominator = denominator + jnp.sum(weights, axis=1, keepdims=True)
        context = context + jnp.dot(
            weights.astype(jnp.bfloat16), ref[:, :LAT], preferred_element_type=jnp.float32
        )
    context = (context / denominator).astype(jnp.bfloat16)
    for h in range(HEADS_HERE):
        out_ref[:, h * VDIM : (h + 1) * VDIM] = jnp.dot(
            context[h * TOK : (h + 1) * TOK], lift_ref[h], preferred_element_type=jnp.float32
        ).astype(jnp.bfloat16)


def project_kernel(lifted_ref, proj_ref, out_ref):
    lifted = lifted_ref[...]
    for pair in range(N_Y // 2):
        weights = jnp.concatenate([proj_ref[2 * pair], proj_ref[2 * pair + 1]], axis=1)
        full = jnp.dot(lifted, weights, preferred_element_type=jnp.float32).astype(jnp.bfloat16)
        for side in range(2):
            for x in range(N_X):
                for p in range(2):
                    row = x * TOK + p * HALF
                    out_ref[x * 16 + (2 * pair + side) * 2 + p] = full[
                        row : row + HALF, side * 128 : (side + 1) * 128
                    ]


def hidden_kernel(steps, rows_ref, gate_ref, up_ref, out_ref, acc_ref, square_ref):
    step = pl.program_id(0)

    @pl.when(step == 0)
    def _():
        acc_ref[...] = jnp.zeros_like(acc_ref)
        square_ref[...] = jnp.zeros_like(square_ref)

    total = acc_ref[...]
    squares = square_ref[...]
    for i in range(rows_ref.shape[0]):
        rows = rows_ref[i]
        weights = jnp.concatenate(
            [gate_ref[i * 256 : (i + 1) * 256], up_ref[i * 256 : (i + 1) * 256]], axis=1
        )
        total = total + jnp.dot(rows, weights, preferred_element_type=jnp.float32)
        wide = rows.astype(jnp.float32)
        wide = wide * wide
        squares = squares + (wide[:, :128] + wide[:, 128:])
    acc_ref[...] = total
    square_ref[...] = squares

    @pl.when(step == steps - 1)
    def _():
        mean = jnp.sum(square_ref[...], axis=1, keepdims=True) / D
        inverse = lax.rsqrt(mean + 1e-06)
        gate = acc_ref[:, :128] * inverse
        up = acc_ref[:, 128:] * inverse
        out_ref[...] = (gate / (1.0 + jnp.exp(-gate)) * up).astype(jnp.bfloat16)


def down_kernel(steps, act_ref, down_ref, out_ref, acc_ref):
    step = pl.program_id(0)

    @pl.when(step == 0)
    def _():
        acc_ref[...] = jnp.zeros_like(acc_ref)

    parts = act_ref.shape[0]
    wide = jnp.concatenate([act_ref[i] for i in range(parts)], axis=1)
    acc_ref[...] += jnp.dot(wide, down_ref[...], preferred_element_type=jnp.float32)

    @pl.when(step == steps - 1)
    def _():
        out_ref[...] = acc_ref[...].astype(jnp.bfloat16)


def attend(place, queries, own, other, value_up):
    return pl.pallas_call(
        attention_kernel,
        out_shape=jax.ShapeDtypeStruct((TOK, HEADS_HERE * VDIM), jnp.bfloat16),
        in_specs=[pl.BlockSpec(memory_space=pltpu.SMEM)]
        + [pl.BlockSpec(memory_space=pltpu.VMEM)] * 4,
        out_specs=pl.BlockSpec(memory_space=pltpu.VMEM),
        name="attend",
    )(place, queries, own, other, value_up)


def project(lifted, proj):
    return pl.pallas_call(
        project_kernel,
        out_shape=jax.ShapeDtypeStruct((64, HALF, 128), jnp.bfloat16),
        name="project",
    )(lifted, proj)


def hidden(rows, w_gate, w_up):
    steps = 4
    per = N_HEAD // steps
    return pl.pallas_call(
        functools.partial(hidden_kernel, steps),
        out_shape=jax.ShapeDtypeStruct((SLOTS, 128), jnp.bfloat16),
        grid=(steps,),
        in_specs=[
            pl.BlockSpec((per, SLOTS, 256), lambda i: (i, 0, 0)),
            pl.BlockSpec((per * 256, 128), lambda i: (i, 0)),
            pl.BlockSpec((per * 256, 128), lambda i: (i, 0)),
        ],
        out_specs=pl.BlockSpec((SLOTS, 128), lambda i: (0, 0)),
        scratch_shapes=[
            pltpu.VMEM((SLOTS, 256), jnp.float32),
            pltpu.VMEM((SLOTS, 128), jnp.float32),
        ],
        name="hidden",
    )(rows, w_gate, w_up)


def down(act, w_down):
    steps = 2
    per = N_HEAD // steps
    return pl.pallas_call(
        functools.partial(down_kernel, steps),
        out_shape=jax.ShapeDtypeStruct((SLOTS, 256), jnp.bfloat16),
        grid=(steps,),
        in_specs=[
            pl.BlockSpec((per, SLOTS, 128), lambda i: (i, 0, 0)),
            pl.BlockSpec((per * 128, 256), lambda i: (i, 0)),
        ],
        out_specs=pl.BlockSpec((SLOTS, 256), lambda i: (0, 0)),
        scratch_shapes=[pltpu.VMEM((SLOTS, 256), jnp.float32)],
        name="down",
    )(act, w_down)


def per_device(
    tokens, queries, latents, value_up, out_proj, expert_ids, expert_gates, w_gate, w_up, w_down
):
    blk = lax.axis_index("blk")
    core = lax.axis_index("head") & 1

    half = lax.dynamic_slice(latents, (core * HALF, 0), (HALF, LAT + ROPE))
    own = lax.all_to_all(
        jnp.broadcast_to(half[None], (N_BLK,) + half.shape), "blk", 0, 0, tiled=True
    ).reshape(KEYS, LAT + ROPE)
    other = lax.ppermute(own, "head", CORE_SWAP)

    proj = lax.all_gather(
        out_proj, "blk", axis=0, tiled=True, axis_index_groups=Y_GROUPS
    ).reshape(N_Y, out_proj.shape[0], 128)

    place = jnp.stack([blk, core]).astype(jnp.int32)
    lifted = attend(place, queries, own, other, value_up)

    lifted_row = lax.all_to_all(
        jnp.broadcast_to(lifted[None], (N_X,) + lifted.shape),
        "blk",
        0,
        0,
        tiled=True,
        axis_index_groups=X_GROUPS,
    ).reshape(N_X * TOK, lifted.shape[1])
    partial = project(lifted_row, proj)
    spread = lax.all_to_all(
        partial, ("blk", "head"), 0, 0, tiled=True, axis_index_groups=XH_GROUPS
    )
    summed = jnp.sum(spread.reshape(N_X, N_HEAD, HALF, 128).astype(jnp.float32), axis=1)
    keep = lax.dynamic_slice(summed, (2 * core, 0, 0), (2, HALF, 128))
    send = lax.dynamic_slice(summed, (2 - 2 * core, 0, 0), (2, HALF, 128))
    got = lax.ppermute(send, "head", CORE_SWAP)
    top = jnp.where(core == 0, keep, got)
    bottom = jnp.where(core == 0, got, keep)
    attended = jnp.concatenate([top, bottom], axis=1)
    attended = jnp.concatenate([attended[0], attended[1]], axis=1)
    mid_state = (tokens.astype(jnp.float32) + attended).astype(jnp.bfloat16)
    mid_wide = mid_state.astype(jnp.float32)

    row_count = tokens.shape[0]
    flat_ids = expert_ids.reshape(-1)
    choose_count = expert_ids.shape[1]
    onehot_ids = (flat_ids[:, None] == jnp.arange(EXPERTS, dtype=jnp.int32)[None, :]).astype(
        jnp.int32
    )
    earlier = jnp.cumsum(onehot_ids, axis=0) - onehot_ids
    ranks = jnp.sum(earlier * onehot_ids, axis=1)
    slot_ids = flat_ids * CAP + ranks
    slot_hits = jnp.arange(SLOTS, dtype=jnp.int32)[:, None] == slot_ids[None, :]
    select = jnp.sum(
        slot_hits.astype(jnp.bfloat16).reshape(SLOTS, row_count, choose_count), axis=2
    )
    combine = jnp.sum(
        jnp.where(slot_hits, expert_gates.reshape(-1)[None, :], 0.0).reshape(
            SLOTS, row_count, choose_count
        ),
        axis=2,
    )

    outgoing = (
        jnp.dot(select, mid_state, preferred_element_type=jnp.float32)
        .astype(jnp.bfloat16)
        .reshape(EXPERTS, CAP, 256)
    )
    incoming = lax.all_to_all(outgoing, "blk", split_axis=0, concat_axis=0, tiled=True)
    rows = lax.all_gather(incoming.reshape(SLOTS, 256), "head", axis=0, tiled=True)
    act = hidden(rows.reshape(N_HEAD, SLOTS, 256), w_gate[0], w_up[0])
    acts = lax.all_gather(act, "head", axis=0, tiled=True)
    expert_out = down(acts.reshape(N_HEAD, SLOTS, 128), w_down[0])
    returned = lax.all_to_all(
        expert_out.reshape(EXPERTS, CAP, 256), "blk", split_axis=0, concat_axis=0, tiled=True
    )
    returned_wide = returned.reshape(SLOTS, 256).astype(jnp.float32)
    routed = jnp.einsum("sr,sd->rd", combine, returned_wide, precision=lax.Precision.HIGHEST)
    return (mid_wide + routed).astype(jnp.bfloat16)


def solution(mesh):
    placed = (
        P("blk", "head"),
        P("blk", "head"),
        P("blk", None),
        P("head", None, None),
        P("head", "blk"),
        P("blk", None),
        P("blk", None),
        P("blk", None, "head"),
        P("blk", None, "head"),
        P("blk", None, "head"),
    )
    return jax.shard_map(
        per_device, mesh=mesh, in_specs=placed, out_specs=P("blk", "head"), check_vma=False
    )
```

```python
import functools

import jax
import jax.numpy as jnp
from jax import lax
from jax.experimental import pallas as pl
from jax.experimental.pallas import tpu as pltpu
from jax.sharding import PartitionSpec as P

D = 4096
LAT = 512
ROPE = 64
QKNOPE = 128
VDIM = 128
EXPERTS = 32
CAP = 20
SLOTS = EXPERTS * CAP
TOK = 64
HALF = TOK // 2
N_BLK = 32
N_HEAD = 16
N_X = 4
N_Y = 8
HEADS_HERE = 4
KEYS = N_BLK * HALF
SCALE = (QKNOPE + ROPE) ** (-0.5)

X_GROUPS = [[y * N_X + x for x in range(N_X)] for y in range(N_Y)]
Y_GROUPS = [[y * N_X + x for y in range(N_Y)] for x in range(N_X)]
XH_GROUPS = [[y * 64 + i for i in range(64)] for y in range(N_Y)]
QUAD = 4
PART = CAP // QUAD
ROWS = N_BLK * PART
QUADS = [[q * QUAD + i for i in range(QUAD)] for q in range(N_HEAD // QUAD)]
ACROSS = [[q * QUAD + i for q in range(N_HEAD // QUAD)] for i in range(QUAD)]
BLK_QUAD = [
    [b * N_HEAD + q * QUAD + i for b in range(N_BLK) for i in range(QUAD)]
    for q in range(N_HEAD // QUAD)
]
CORE_SWAP = [(i, i ^ 1) for i in range(N_HEAD)]
CHIP_SWAP = [(i, i ^ 2) for i in range(N_HEAD)]
Y_SWAPS = [[(b, b ^ (N_X * k)) for b in range(N_BLK)] for k in range(N_Y)]


def attention_kernel(place_ref, q_ref, own_ref, other_ref, lift_ref, out_ref):
    width = LAT + ROPE
    q_all = q_ref[...]
    q_rows = jnp.concatenate(
        [q_all[:, h * width : (h + 1) * width] for h in range(HEADS_HERE)], axis=0
    )
    rows = HEADS_HERE * TOK
    first = place_ref[0] * TOK
    core = place_ref[1]
    query_pos = first + (lax.broadcasted_iota(jnp.int32, (rows, N_Y * HALF), 0) & (TOK - 1))
    key_idx = lax.broadcasted_iota(jnp.int32, (rows, N_Y * HALF), 1)
    room = query_pos - ((key_idx >> 5) * (N_X * TOK) + (key_idx & (HALF - 1)))
    chunks = [
        (ref, x, x * TOK + part * HALF)
        for part, ref in ((core, own_ref), (1 - core, other_ref))
        for x in range(N_X)
    ]
    scores = []
    row_max = None
    for ref, x, offset in chunks:
        raw = jnp.dot(q_rows, ref[x], preferred_element_type=jnp.float32)
        raw = jnp.where(room >= offset, raw * SCALE, -1e30)
        scores.append(raw)
        row_max = raw if row_max is None else jnp.maximum(row_max, raw)
    row_max = jnp.max(row_max, axis=1, keepdims=True)
    total = 0.0
    context = 0.0
    for (ref, x, offset), raw in zip(chunks, scores):
        weights = jnp.where(room >= offset, jnp.exp(raw - row_max), 0.0)
        total = total + weights
        context = context + lax.dot_general(
            weights.astype(jnp.bfloat16),
            ref[x, :LAT],
            (((1,), (1,)), ((), ())),
            preferred_element_type=jnp.float32,
        )
    denominator = jnp.sum(total, axis=1, keepdims=True)
    context = (context / denominator).astype(jnp.bfloat16)
    for h in range(HEADS_HERE):
        lifted = jnp.dot(
            context[h * TOK : (h + 1) * TOK], lift_ref[h], preferred_element_type=jnp.float32
        ).astype(jnp.bfloat16)
        for x in range(N_X):
            out_ref[x, :, h * VDIM : (h + 1) * VDIM] = lifted


def project_kernel(place_ref, lifted_ref, *refs):
    proj_refs, out_ref = refs[:N_Y], refs[N_Y]
    lifted = lifted_ref[...]
    y = place_ref[0] // N_X
    for pair in range(N_Y // 2):
        weights = jnp.concatenate(
            [proj_refs[2 * pair][...], proj_refs[2 * pair + 1][...]], axis=1
        )
        full = jnp.dot(lifted, weights, preferred_element_type=jnp.float32).astype(jnp.bfloat16)
        for side in range(2):
            target = jnp.bitwise_xor(y, 2 * pair + side)
            for x in range(N_X):
                for p in range(2):
                    row = x * TOK + p * HALF
                    out_ref[x * 16 + target * 2 + p] = full[
                        row : row + HALF, side * 128 : (side + 1) * 128
                    ]


def hidden_kernel(place_ref, rows_ref, *refs):
    weight_refs, (out_ref, acc_ref, square_ref) = refs[:QUAD], refs[QUAD:]
    step = pl.program_id(0)

    @pl.when(step == 0)
    def _():
        acc_ref[...] = jnp.zeros_like(acc_ref)
        square_ref[...] = jnp.zeros_like(square_ref)

    rows = rows_ref[step]
    for j in range(QUAD):
        acc_ref[j] += jnp.dot(rows, weight_refs[j][...], preferred_element_type=jnp.float32)
    wide = rows.astype(jnp.float32)
    square_ref[...] += jnp.sum(wide * wide, axis=1, keepdims=True)

    @pl.when(step == QUAD - 1)
    def _():
        inverse = lax.rsqrt(square_ref[...] / D + 1e-06)
        for j in range(QUAD):
            owner = jnp.bitwise_xor(place_ref[2], j)
            gate = acc_ref[j, :, :128] * inverse
            up = acc_ref[j, :, 128:] * inverse
            act = (gate / (1.0 + jnp.exp(-gate)) * up).astype(jnp.bfloat16)
            for other in range(QUAD):

                @pl.when(owner == other)
                def _():
                    for q in range(QUAD):
                        out_ref[q, :, other * 128 : (other + 1) * 128] = act


def down_kernel(place_ref, act_ref, *refs):
    weight_refs, out_ref = refs[:QUAD], refs[QUAD]
    wide = jnp.concatenate([act_ref[i] for i in range(QUAD)], axis=1)
    for j in range(QUAD):
        owner = jnp.bitwise_xor(place_ref[2], j)
        result = jnp.dot(wide, weight_refs[j][...], preferred_element_type=jnp.float32).astype(
            jnp.bfloat16
        )
        for other in range(QUAD):

            @pl.when(owner == other)
            def _():
                out_ref[:, other * 256 : (other + 1) * 256] = result


def attend(place, queries, own, other, value_up):
    return pl.pallas_call(
        attention_kernel,
        out_shape=jax.ShapeDtypeStruct((N_X, TOK, HEADS_HERE * VDIM), jnp.bfloat16),
        in_specs=[pl.BlockSpec(memory_space=pltpu.SMEM)]
        + [pl.BlockSpec(memory_space=pltpu.VMEM)] * 4,
        out_specs=pl.BlockSpec(memory_space=pltpu.VMEM),
        name="attend",
    )(place, queries, own, other, value_up)


def project(place, lifted, proj):
    return pl.pallas_call(
        project_kernel,
        out_shape=jax.ShapeDtypeStruct((64, HALF, 128), jnp.bfloat16),
        in_specs=[pl.BlockSpec(memory_space=pltpu.SMEM)]
        + [pl.BlockSpec(memory_space=pltpu.VMEM)] * (1 + N_Y),
        out_specs=pl.BlockSpec(memory_space=pltpu.VMEM),
        name="project",
    )(place, lifted, *proj)


def hidden(place, rows, weights):
    depth = D // QUAD
    return pl.pallas_call(
        hidden_kernel,
        out_shape=jax.ShapeDtypeStruct((QUAD, ROWS, QUAD * 128), jnp.bfloat16),
        grid=(QUAD,),
        in_specs=[
            pl.BlockSpec(memory_space=pltpu.SMEM),
            pl.BlockSpec(memory_space=pltpu.VMEM),
        ]
        + [pl.BlockSpec((depth, 256), lambda i: (i, 0))] * QUAD,
        out_specs=pl.BlockSpec((QUAD, ROWS, QUAD * 128), lambda i: (0, 0, 0)),
        scratch_shapes=[
            pltpu.VMEM((QUAD, ROWS, 256), jnp.float32),
            pltpu.VMEM((ROWS, 1), jnp.float32),
        ],
        name="hidden",
    )(place, rows, *weights)


def down(place, act, weights):
    depth = QUAD * QUAD * 128
    return pl.pallas_call(
        down_kernel,
        out_shape=jax.ShapeDtypeStruct((ROWS, QUAD * 256), jnp.bfloat16),
        grid=(1,),
        in_specs=[
            pl.BlockSpec(memory_space=pltpu.SMEM),
            pl.BlockSpec(memory_space=pltpu.VMEM),
        ]
        + [pl.BlockSpec((depth, 256), lambda i: (D // depth, 0))] * QUAD,
        out_specs=pl.BlockSpec((ROWS, QUAD * 256), lambda i: (0, 0)),
        name="down",
    )(place, act, *weights)


def spread_over(x, axis, groups):
    count = len(groups[0])
    return lax.all_to_all(
        jnp.broadcast_to(x[None], (count,) + x.shape), axis, 0, 0, tiled=True, axis_index_groups=groups
    )


def per_device(
    tokens, queries, latents, value_up, out_proj, expert_ids, expert_gates, w_gate, w_up, w_down
):
    blk = lax.axis_index("blk")
    core = lax.axis_index("head") & 1

    weights = jnp.concatenate([jnp.concatenate([w_gate[0], w_up[0]], axis=1), w_down[0]], axis=0)
    weights_chip = lax.ppermute(weights, "head", CHIP_SWAP)
    weights_core = lax.ppermute(weights, "head", CORE_SWAP)
    weights_both = lax.ppermute(weights_chip, "head", CORE_SWAP)
    quad_weights = (weights, weights_core, weights_chip, weights_both)

    proj = [out_proj] + [lax.ppermute(out_proj, "blk", Y_SWAPS[j]) for j in range(1, N_Y)]

    half = lax.dynamic_slice(latents, (core * HALF, 0), (HALF, LAT + ROPE))
    column = spread_over(half, "blk", Y_GROUPS).reshape(N_Y * HALF, LAT + ROPE).T
    column, *proj[1:4] = lax.optimization_barrier((column, *proj[1:4]))
    own = spread_over(column, "blk", X_GROUPS).reshape(N_X, LAT + ROPE, N_Y * HALF)
    own, *proj[4:] = lax.optimization_barrier((own, *proj[4:]))
    other = lax.ppermute(own, "head", CORE_SWAP)

    place = jnp.stack([blk, core, lax.axis_index("head") & (QUAD - 1)]).astype(jnp.int32)
    lifted = attend(place, queries, own, other, value_up)

    lifted_row = lax.all_to_all(
        lifted, "blk", 0, 0, tiled=True, axis_index_groups=X_GROUPS
    ).reshape(N_X * TOK, lifted.shape[2])
    partial = project(place, lifted_row, proj)
    spread = lax.all_to_all(
        partial, ("blk", "head"), 0, 0, tiled=True, axis_index_groups=XH_GROUPS
    )
    summed = jnp.sum(spread.reshape(N_X, N_HEAD, HALF, 128).astype(jnp.float32), axis=1)
    keep = lax.dynamic_slice(summed, (2 * core, 0, 0), (2, HALF, 128))
    send = lax.dynamic_slice(summed, (2 - 2 * core, 0, 0), (2, HALF, 128))
    got = lax.ppermute(send, "head", CORE_SWAP)
    top = jnp.where(core == 0, keep, got)
    bottom = jnp.where(core == 0, got, keep)
    attended = jnp.concatenate([top, bottom], axis=1)
    attended = jnp.concatenate([attended[0], attended[1]], axis=1)
    mid_state = (tokens.astype(jnp.float32) + attended).astype(jnp.bfloat16)
    mid_wide = mid_state.astype(jnp.float32)

    row_count = tokens.shape[0]
    flat_ids = expert_ids.reshape(-1)
    choose_count = expert_ids.shape[1]
    onehot_ids = (flat_ids[:, None] == jnp.arange(EXPERTS, dtype=jnp.int32)[None, :]).astype(
        jnp.int32
    )
    earlier = jnp.cumsum(onehot_ids, axis=0) - onehot_ids
    ranks = jnp.sum(earlier * onehot_ids, axis=1)
    slot_ids = flat_ids * CAP + ranks
    slot_hits = jnp.arange(SLOTS, dtype=jnp.int32)[:, None] == slot_ids[None, :]
    select = jnp.sum(
        slot_hits.astype(jnp.bfloat16).reshape(SLOTS, row_count, choose_count), axis=2
    )
    combine = jnp.sum(
        jnp.where(slot_hits, expert_gates.reshape(-1)[None, :], 0.0).reshape(
            SLOTS, row_count, choose_count
        ),
        axis=2,
    )

    outgoing = (
        jnp.dot(select, mid_state, preferred_element_type=jnp.float32)
        .astype(jnp.bfloat16)
        .reshape(N_BLK * QUAD, PART * 2, 128)
    )
    incoming = lax.all_to_all(
        outgoing, ("blk", "head"), 0, 0, tiled=True, axis_index_groups=BLK_QUAD
    )
    rows_here = (
        incoming.reshape(N_BLK, QUAD, PART, 256).transpose(0, 2, 1, 3).reshape(ROWS, QUAD * 256)
    )
    rows = spread_over(rows_here, "head", ACROSS).reshape(QUAD, ROWS, QUAD * 256)
    act = hidden(place, rows, quad_weights)
    acts = lax.all_to_all(act, "head", 0, 0, tiled=True, axis_index_groups=ACROSS)
    expert_out = down(place, acts, quad_weights)
    sent = (
        expert_out.reshape(N_BLK, PART, QUAD, 256)
        .transpose(0, 2, 1, 3)
        .reshape(N_BLK * QUAD, PART * 2, 128)
    )
    returned = lax.all_to_all(
        sent, ("blk", "head"), 0, 0, tiled=True, axis_index_groups=BLK_QUAD
    )
    returned_wide = returned.reshape(SLOTS, 256).astype(jnp.float32)
    routed = jnp.einsum("sr,sd->rd", combine, returned_wide, precision=lax.Precision.HIGHEST)
    return (mid_wide + routed).astype(jnp.bfloat16)


def solution(mesh):
    placed = (
        P("blk", "head"),
        P("blk", "head"),
        P("blk", None),
        P("head", None, None),
        P("head", "blk"),
        P("blk", None),
        P("blk", None),
        P("blk", None, "head"),
        P("blk", None, "head"),
        P("blk", None, "head"),
    )
    return jax.shard_map(
        per_device, mesh=mesh, in_specs=placed, out_specs=P("blk", "head"), check_vma=False
    )
```

```python
import jax
import jax.numpy as jnp
from jax import lax
from jax.experimental import pallas as pl
from jax.experimental.pallas import tpu as pltpu
from jax.sharding import PartitionSpec as P


D = 4096
LAT = 512
ROPE = 64
QKNOPE = 128
VDIM = 128
EXPERTS = 32
CAP = 20
SLOTS = EXPERTS * CAP
TOK = 64
HALF = TOK // 2
N_BLK = 32
N_HEAD = 16
N_X = 4
N_Y = 8
HEADS_HERE = 4
SCALE = (QKNOPE + ROPE) ** (-0.5)

X_GROUPS = [[y * N_X + x for x in range(N_X)] for y in range(N_Y)]
Y_GROUPS = [[y * N_X + x for y in range(N_Y)] for x in range(N_X)]
N_Z = N_HEAD // 2


def device(y, x, z, core):
    return (y * N_X + x) * N_HEAD + z * 2 + core


XC_GROUPS = [
    [device(y, x, z, c) for x in range(N_X) for c in range(2)]
    for y in range(N_Y)
    for z in range(N_Z)
]
XZ_GROUPS = [
    [device(y, x, z, c) for x in range(N_X) for z in range(N_Z)]
    for y in range(N_Y)
    for c in range(2)
]
PROJ_MOVE = [
    (device(y, x, z, c), device((y & 6) | c, x, z, y & 1))
    for y in range(N_Y)
    for x in range(N_X)
    for z in range(N_Z)
    for c in range(2)
]
QUAD = 4
PART = CAP // QUAD
ROWS = N_BLK * PART
QUADS = [[q * QUAD + i for i in range(QUAD)] for q in range(N_HEAD // QUAD)]
ACROSS = [[q * QUAD + i for q in range(N_HEAD // QUAD)] for i in range(QUAD)]
BLK_QUAD = [
    [b * N_HEAD + q * QUAD + i for b in range(N_BLK) for i in range(QUAD)]
    for q in range(N_HEAD // QUAD)
]
CORE_SWAP = [(i, i ^ 1) for i in range(N_HEAD)]
CHIP_SWAP = [(i, i ^ 2) for i in range(N_HEAD)]
BOTH_SWAP = [(i, i ^ 3) for i in range(N_HEAD)]


def attention_kernel(place_ref, q_ref, own_ref, other_ref, lift_ref, out_ref):
    width = LAT + ROPE
    q_all = q_ref[...]
    q_rows = jnp.concatenate(
        [q_all[:, h * width : (h + 1) * width] for h in range(HEADS_HERE)], axis=0
    )
    rows = HEADS_HERE * TOK
    first = place_ref[0] * TOK
    core = place_ref[1]
    query_pos = first + (lax.broadcasted_iota(jnp.int32, (rows, N_Y * HALF), 0) & (TOK - 1))
    key_idx = lax.broadcasted_iota(jnp.int32, (rows, N_Y * HALF), 1)
    room = query_pos - ((key_idx >> 5) * (N_X * TOK) + (key_idx & (HALF - 1)))
    chunks = [
        (ref, x, x * TOK + part * HALF)
        for part, ref in ((core, own_ref), (1 - core, other_ref))
        for x in range(N_X)
    ]
    scores = []
    row_max = None
    for ref, x, offset in chunks:
        raw = jnp.dot(q_rows, ref[x], preferred_element_type=jnp.float32)
        raw = jnp.where(room >= offset, raw * SCALE, -1e30)
        scores.append(raw)
        row_max = raw if row_max is None else jnp.maximum(row_max, raw)
    row_max = jnp.max(row_max, axis=1, keepdims=True)
    total = 0.0
    context = 0.0
    for (ref, x, offset), raw in zip(chunks, scores):
        weights = jnp.where(room >= offset, jnp.exp(raw - row_max), 0.0)
        total = total + weights
        context = context + lax.dot_general(
            weights.astype(jnp.bfloat16),
            ref[x, :LAT],
            (((1,), (1,)), ((), ())),
            preferred_element_type=jnp.float32,
        )
    denominator = jnp.sum(total, axis=1, keepdims=True)
    context = (context / denominator).astype(jnp.bfloat16)
    for h in range(HEADS_HERE):
        lifted = jnp.dot(
            context[h * TOK : (h + 1) * TOK], lift_ref[h], preferred_element_type=jnp.float32
        ).astype(jnp.bfloat16)
        for member in range(2 * N_X):
            out_ref[member, :, h * VDIM : (h + 1) * VDIM] = lifted


def project_kernel(lifted_ref, proj_ref, out_ref):
    halves = [
        jnp.concatenate([lifted_ref[x * 2 + c] for x in range(N_X)], axis=0) for c in range(2)
    ]
    lifted = jnp.concatenate(halves, axis=1)
    for pair in range(N_Y // 4):
        weights = jnp.concatenate([proj_ref[2 * pair], proj_ref[2 * pair + 1]], axis=1)
        full = jnp.dot(lifted, weights, preferred_element_type=jnp.float32).astype(jnp.bfloat16)
        for side in range(2):
            for x in range(N_X):
                for p in range(2):
                    row = x * TOK + p * HALF
                    out_ref[x * N_Z + (2 * pair + side) * 2 + p] = full[
                        row : row + HALF, side * 128 : (side + 1) * 128
                    ]


def mid_kernel(place_ref, attended_ref, *refs):
    token_refs, (quad_ref, own_ref) = refs[:QUAD], refs[QUAD:]
    me = place_ref[2]
    for j in range(QUAD):
        owner = jnp.bitwise_xor(me, j)
        core = owner // 2
        first = (owner % 2) * 2
        for p in range(2):
            rows = slice(p * HALF, (p + 1) * HALF)
            wide = [
                token_refs[j][rows, i * 128 : (i + 1) * 128].astype(jnp.float32)
                + attended_ref[p * 2 + core, first + i]
                for i in range(2)
            ]
            mid = jnp.concatenate(wide, axis=1).astype(jnp.bfloat16)
            if j == 0:
                own_ref[rows, :] = mid
            for other in range(QUAD):

                @pl.when(owner == other)
                def _():
                    quad_ref[rows, other * 256 : (other + 1) * 256] = mid


def hidden_kernel(place_ref, rows_ref, *refs):
    weight_refs, (out_ref, acc_ref, square_ref) = refs[:QUAD], refs[QUAD:]
    step = pl.program_id(0)

    @pl.when(step == 0)
    def _():
        acc_ref[...] = jnp.zeros_like(acc_ref)
        square_ref[...] = jnp.zeros_like(square_ref)

    rows = rows_ref[step]
    for j in range(QUAD):
        acc_ref[j] += jnp.dot(rows, weight_refs[j][...], preferred_element_type=jnp.float32)
    wide = rows.astype(jnp.float32)
    square_ref[...] += jnp.sum(wide * wide, axis=1, keepdims=True)

    @pl.when(step == QUAD - 1)
    def _():
        inverse = lax.rsqrt(square_ref[...] / D + 1e-06)
        for j in range(QUAD):
            owner = jnp.bitwise_xor(place_ref[2], j)
            gate = acc_ref[j, :, :128] * inverse
            up = acc_ref[j, :, 128:] * inverse
            act = (gate / (1.0 + jnp.exp(-gate)) * up).astype(jnp.bfloat16)
            for other in range(QUAD):

                @pl.when(owner == other)
                def _():
                    for q in range(QUAD):
                        out_ref[q, :, other * 128 : (other + 1) * 128] = act


def down_kernel(place_ref, act_ref, *refs):
    weight_refs, out_ref = refs[:QUAD], refs[QUAD]
    wide = jnp.concatenate([act_ref[i] for i in range(QUAD)], axis=1)
    for j in range(QUAD):
        owner = jnp.bitwise_xor(place_ref[2], j)
        result = jnp.dot(wide, weight_refs[j][...], preferred_element_type=jnp.float32).astype(
            jnp.bfloat16
        )
        for other in range(QUAD):

            @pl.when(owner == other)
            def _():
                out_ref[:, other * 256 : (other + 1) * 256] = result


def attend(place, queries, own, other, value_up):
    return pl.pallas_call(
        attention_kernel,
        out_shape=jax.ShapeDtypeStruct((2 * N_X, TOK, HEADS_HERE * VDIM), jnp.bfloat16),
        in_specs=[pl.BlockSpec(memory_space=pltpu.SMEM)]
        + [pl.BlockSpec(memory_space=pltpu.VMEM)] * 4,
        out_specs=pl.BlockSpec(memory_space=pltpu.VMEM),
        name="attend",
    )(place, queries, own, other, value_up)


def project(lifted, proj):
    return pl.pallas_call(
        project_kernel,
        out_shape=jax.ShapeDtypeStruct((N_X * N_Z, HALF, 128), jnp.bfloat16),
        in_specs=[pl.BlockSpec(memory_space=pltpu.VMEM)] * 2,
        out_specs=pl.BlockSpec(memory_space=pltpu.VMEM),
        name="project",
    )(lifted, proj)


def middle(place, attended, tokens):
    return pl.pallas_call(
        mid_kernel,
        out_shape=(
            jax.ShapeDtypeStruct((TOK, QUAD * 256), jnp.bfloat16),
            jax.ShapeDtypeStruct((TOK, 256), jnp.bfloat16),
        ),
        in_specs=[pl.BlockSpec(memory_space=pltpu.SMEM)]
        + [pl.BlockSpec(memory_space=pltpu.VMEM)] * (1 + QUAD),
        out_specs=(pl.BlockSpec(memory_space=pltpu.VMEM),) * 2,
        name="middle",
    )(place, attended, *tokens)


def hidden(place, rows, weights):
    depth = D // QUAD
    return pl.pallas_call(
        hidden_kernel,
        out_shape=jax.ShapeDtypeStruct((QUAD, ROWS, QUAD * 128), jnp.bfloat16),
        grid=(QUAD,),
        in_specs=[
            pl.BlockSpec(memory_space=pltpu.SMEM),
            pl.BlockSpec(memory_space=pltpu.VMEM),
        ]
        + [pl.BlockSpec((depth, 256), lambda i: (i, 0))] * QUAD,
        out_specs=pl.BlockSpec((QUAD, ROWS, QUAD * 128), lambda i: (0, 0, 0)),
        scratch_shapes=[
            pltpu.VMEM((QUAD, ROWS, 256), jnp.float32),
            pltpu.VMEM((ROWS, 1), jnp.float32),
        ],
        name="hidden",
    )(place, rows, *weights)


def down(place, act, weights):
    return pl.pallas_call(
        down_kernel,
        out_shape=jax.ShapeDtypeStruct((ROWS, QUAD * 256), jnp.bfloat16),
        in_specs=[pl.BlockSpec(memory_space=pltpu.SMEM)]
        + [pl.BlockSpec(memory_space=pltpu.VMEM)] * (1 + QUAD),
        out_specs=pl.BlockSpec(memory_space=pltpu.VMEM),
        name="down",
    )(place, act, *weights)


def spread_over(x, axis, groups):
    count = len(groups[0])
    return lax.all_to_all(
        jnp.broadcast_to(x[None], (count,) + x.shape), axis, 0, 0, tiled=True, axis_index_groups=groups
    )


def quad_of(own, chip):
    core = lax.ppermute(own, "head", CORE_SWAP)
    return (own, core, chip, lax.ppermute(chip, "head", CORE_SWAP))


def per_device(
    tokens, queries, latents, value_up, out_proj, expert_ids, expert_gates, w_gate, w_up, w_down
):
    blk = lax.axis_index("blk")
    core = lax.axis_index("head") & 1

    quad_tokens = [tokens] + [
        lax.ppermute(tokens, "head", swap) for swap in (CORE_SWAP, CHIP_SWAP, BOTH_SWAP)
    ]
    moved = lax.ppermute(out_proj, ("blk", "head"), PROJ_MOVE)
    proj = lax.all_gather(moved, "blk", axis=0, tiled=True, axis_index_groups=Y_GROUPS)
    proj = proj.reshape(N_Y // 2, 2 * out_proj.shape[0], 128)

    half = lax.dynamic_slice(latents, (core * HALF, 0), (HALF, LAT + ROPE))
    column = spread_over(half, "blk", Y_GROUPS).reshape(N_Y * HALF, LAT + ROPE).T
    column, *quad_tokens[1:] = lax.optimization_barrier((column, *quad_tokens[1:]))

    gate_up = jnp.concatenate([w_gate[0], w_up[0]], axis=1)
    gate_up_chip = lax.ppermute(gate_up, "head", CHIP_SWAP)
    down_chip = lax.ppermute(w_down[0], "head", CHIP_SWAP)
    gate_up_quad = quad_of(gate_up, gate_up_chip)
    down_quad = quad_of(w_down[0], down_chip)

    own = spread_over(column, "blk", X_GROUPS).reshape(N_X, LAT + ROPE, N_Y * HALF)
    other = lax.ppermute(own, "head", CORE_SWAP)

    place = jnp.stack([blk, core, lax.axis_index("head") & (QUAD - 1)]).astype(jnp.int32)
    lifted = attend(place, queries, own, other, value_up)

    lifted_row = lax.all_to_all(
        lifted, ("blk", "head"), 0, 0, tiled=True, axis_index_groups=XC_GROUPS
    )
    partial = project(lifted_row, proj)
    spread = lax.all_to_all(partial, ("blk", "head"), 0, 0, tiled=True, axis_index_groups=XZ_GROUPS)
    summed = jnp.sum(spread.reshape(N_X, N_Z, HALF, 128).astype(jnp.float32), axis=1)
    attended = spread_over(summed, "head", QUADS).reshape(QUAD, N_X, HALF, 128)
    mid_quad, mid_state = middle(place, attended, quad_tokens)
    mid_wide = mid_state.astype(jnp.float32)

    row_count = tokens.shape[0]
    flat_ids = expert_ids.reshape(-1)
    choose_count = expert_ids.shape[1]
    onehot_ids = (flat_ids[:, None] == jnp.arange(EXPERTS, dtype=jnp.int32)[None, :]).astype(
        jnp.int32
    )
    earlier = jnp.cumsum(onehot_ids, axis=0) - onehot_ids
    ranks = jnp.sum(earlier * onehot_ids, axis=1)
    slot_ids = flat_ids * CAP + ranks
    slot_hits = jnp.arange(SLOTS, dtype=jnp.int32)[:, None] == slot_ids[None, :]
    row_ids = jnp.arange(ROWS, dtype=jnp.int32)
    row_slots = row_ids // PART * CAP + place[2] * PART + row_ids % PART
    row_hits = row_slots[:, None] == slot_ids[None, :]
    select = jnp.sum(
        row_hits.astype(jnp.bfloat16).reshape(ROWS, row_count, choose_count), axis=2
    )
    combine = jnp.sum(
        jnp.where(slot_hits, expert_gates.reshape(-1)[None, :], 0.0).reshape(
            SLOTS, row_count, choose_count
        ),
        axis=2,
    )

    outgoing = (
        jnp.dot(select, mid_quad, preferred_element_type=jnp.float32)
        .astype(jnp.bfloat16)
        .reshape(N_BLK, PART * QUAD * 2, 128)
    )
    incoming = lax.all_to_all(outgoing, "blk", 0, 0, tiled=True)
    rows_here = incoming.reshape(ROWS, QUAD * 256)
    rows = spread_over(rows_here, "head", ACROSS).reshape(QUAD, ROWS, QUAD * 256)
    act = hidden(place, rows, gate_up_quad)
    acts = lax.all_to_all(act, "head", 0, 0, tiled=True, axis_index_groups=ACROSS)
    expert_out = down(place, acts, down_quad)
    sent = (
        expert_out.reshape(N_BLK, PART, QUAD, 256)
        .transpose(0, 2, 1, 3)
        .reshape(N_BLK * QUAD, PART * 2, 128)
    )
    returned = lax.all_to_all(
        sent, ("blk", "head"), 0, 0, tiled=True, axis_index_groups=BLK_QUAD
    )
    returned_wide = returned.reshape(SLOTS, 256).astype(jnp.float32)
    routed = jnp.einsum("sr,sd->rd", combine, returned_wide, precision=lax.Precision.HIGHEST)
    return (mid_wide + routed).astype(jnp.bfloat16)


def solution(mesh):
    placed = (
        P("blk", "head"),
        P("blk", "head"),
        P("blk", None),
        P("head", None, None),
        P("head", "blk"),
        P("blk", None),
        P("blk", None),
        P("blk", None, "head"),
        P("blk", None, "head"),
        P("blk", None, "head"),
    )

    return jax.shard_map(
        per_device, mesh=mesh, in_specs=placed, out_specs=P("blk", "head"), check_vma=False
    )
```

```python
import jax
import jax.numpy as jnp
from jax import lax
from jax.experimental import pallas as pl
from jax.experimental.pallas import tpu as pltpu
from jax.sharding import PartitionSpec as P


D = 4096
LAT = 512
ROPE = 64
QKNOPE = 128
VDIM = 128
EXPERTS = 32
CAP = 20
SLOTS = EXPERTS * CAP
TOK = 64
HALF = TOK // 2
N_BLK = 32
N_HEAD = 16
N_X = 4
N_Y = 8
HEADS_HERE = 4
SCALE = (QKNOPE + ROPE) ** (-0.5)

X_GROUPS = [[y * N_X + x for x in range(N_X)] for y in range(N_Y)]
Y_GROUPS = [[y * N_X + x for y in range(N_Y)] for x in range(N_X)]
N_Z = N_HEAD // 2


def device(y, x, z, core):
    return (y * N_X + x) * N_HEAD + z * 2 + core


XC_GROUPS = [
    [device(y, x, z, c) for x in range(N_X) for c in range(2)]
    for y in range(N_Y)
    for z in range(N_Z)
]
XZ_GROUPS = [
    [device(y, x, z, c) for x in range(N_X) for z in range(N_Z)]
    for y in range(N_Y)
    for c in range(2)
]
PROJ_MOVE = [
    (device(y, x, z, c), device((y & 6) | c, x, z, y & 1))
    for y in range(N_Y)
    for x in range(N_X)
    for z in range(N_Z)
    for c in range(2)
]
QUAD = 4
PART = CAP // QUAD
ROWS = N_BLK * PART
QUADS = [[q * QUAD + i for i in range(QUAD)] for q in range(N_HEAD // QUAD)]
ACROSS = [[q * QUAD + i for q in range(N_HEAD // QUAD)] for i in range(QUAD)]
BLK_QUAD = [
    [b * N_HEAD + q * QUAD + i for b in range(N_BLK) for i in range(QUAD)]
    for q in range(N_HEAD // QUAD)
]
CORE_SWAP = [(i, i ^ 1) for i in range(N_HEAD)]
CHIP_SWAP = [(i, i ^ 2) for i in range(N_HEAD)]


def attention_kernel(place_ref, q_ref, own_ref, other_ref, lift_ref, out_ref):
    width = LAT + ROPE
    q_all = q_ref[...]
    q_rows = jnp.concatenate(
        [q_all[:, h * width : (h + 1) * width] for h in range(HEADS_HERE)], axis=0
    )
    rows = HEADS_HERE * TOK
    first = place_ref[0] * TOK
    core = place_ref[1]
    query_pos = first + (lax.broadcasted_iota(jnp.int32, (rows, N_Y * HALF), 0) & (TOK - 1))
    key_idx = lax.broadcasted_iota(jnp.int32, (rows, N_Y * HALF), 1)
    room = query_pos - ((key_idx >> 5) * (N_X * TOK) + (key_idx & (HALF - 1)))
    chunks = [
        (ref, x, x * TOK + part * HALF)
        for part, ref in ((core, own_ref), (1 - core, other_ref))
        for x in range(N_X)
    ]
    scores = []
    row_max = None
    for ref, x, offset in chunks:
        raw = jnp.dot(q_rows, ref[x], preferred_element_type=jnp.float32)
        raw = jnp.where(room >= offset, raw * SCALE, -1e30)
        scores.append(raw)
        row_max = raw if row_max is None else jnp.maximum(row_max, raw)
    row_max = jnp.max(row_max, axis=1, keepdims=True)
    total = 0.0
    context = 0.0
    for (ref, x, offset), raw in zip(chunks, scores):
        weights = jnp.where(room >= offset, jnp.exp(raw - row_max), 0.0)
        total = total + weights
        context = context + lax.dot_general(
            weights.astype(jnp.bfloat16),
            ref[x, :LAT],
            (((1,), (1,)), ((), ())),
            preferred_element_type=jnp.float32,
        )
    denominator = jnp.sum(total, axis=1, keepdims=True)
    context = (context / denominator).astype(jnp.bfloat16)
    for h in range(HEADS_HERE):
        lifted = jnp.dot(
            context[h * TOK : (h + 1) * TOK], lift_ref[h], preferred_element_type=jnp.float32
        ).astype(jnp.bfloat16)
        for member in range(2 * N_X):
            out_ref[member, :, h * VDIM : (h + 1) * VDIM] = lifted


def project_kernel(lifted_ref, proj_ref, out_ref):
    halves = [
        jnp.concatenate([lifted_ref[x * 2 + c] for x in range(N_X)], axis=0) for c in range(2)
    ]
    lifted = jnp.concatenate(halves, axis=1)
    for pair in range(N_Y // 4):
        weights = jnp.concatenate([proj_ref[2 * pair], proj_ref[2 * pair + 1]], axis=1)
        full = jnp.dot(lifted, weights, preferred_element_type=jnp.float32).astype(jnp.bfloat16)
        for side in range(2):
            for x in range(N_X):
                for p in range(2):
                    row = x * TOK + p * HALF
                    out_ref[x * N_Z + (2 * pair + side) * 2 + p] = full[
                        row : row + HALF, side * 128 : (side + 1) * 128
                    ]


def mid_kernel(place_ref, shared_ref, quad_ref, own_ref):
    for i in range(QUAD):
        parts = []
        for p in range(2):
            wide = [
                shared_ref[i, 4 + f * 2 + p] + shared_ref[p * 2 + i // 2, i % 2 * 2 + f]
                for f in range(2)
            ]
            parts.append(jnp.concatenate(wide, axis=1))
        mid = jnp.concatenate(parts, axis=0).astype(jnp.bfloat16)
        quad_ref[:, i * 256 : (i + 1) * 256] = mid

        @pl.when(place_ref[2] == i)
        def _():
            own_ref[...] = mid


def hidden_kernel(place_ref, rows_ref, *refs):
    weight_refs, (out_ref, acc_ref, square_ref) = refs[:QUAD], refs[QUAD:]
    step = pl.program_id(0)

    @pl.when(step == 0)
    def _():
        acc_ref[...] = jnp.zeros_like(acc_ref)
        square_ref[...] = jnp.zeros_like(square_ref)

    rows = rows_ref[step]
    for j in range(QUAD):
        acc_ref[j] += jnp.dot(rows, weight_refs[j][...], preferred_element_type=jnp.float32)
    wide = rows.astype(jnp.float32)
    square_ref[...] += jnp.sum(wide * wide, axis=1, keepdims=True)

    @pl.when(step == QUAD - 1)
    def _():
        inverse = lax.rsqrt(square_ref[...] / D + 1e-06)
        for j in range(QUAD):
            owner = jnp.bitwise_xor(place_ref[2], j)
            gate = acc_ref[j, :, :128] * inverse
            up = acc_ref[j, :, 128:] * inverse
            act = (gate / (1.0 + jnp.exp(-gate)) * up).astype(jnp.bfloat16)
            for other in range(QUAD):

                @pl.when(owner == other)
                def _():
                    for q in range(QUAD):
                        out_ref[q, :, other * 128 : (other + 1) * 128] = act


def down_kernel(place_ref, act_ref, *refs):
    weight_refs, out_ref = refs[:QUAD], refs[QUAD]
    wide = jnp.concatenate([act_ref[i] for i in range(QUAD)], axis=1)
    for j in range(QUAD):
        owner = jnp.bitwise_xor(place_ref[2], j)
        result = jnp.dot(wide, weight_refs[j][...], preferred_element_type=jnp.float32).astype(
            jnp.bfloat16
        )
        for other in range(QUAD):

            @pl.when(owner == other)
            def _():
                out_ref[:, other * 256 : (other + 1) * 256] = result


def attend(place, queries, own, other, value_up):
    return pl.pallas_call(
        attention_kernel,
        out_shape=jax.ShapeDtypeStruct((2 * N_X, TOK, HEADS_HERE * VDIM), jnp.bfloat16),
        in_specs=[pl.BlockSpec(memory_space=pltpu.SMEM)]
        + [pl.BlockSpec(memory_space=pltpu.VMEM)] * 4,
        out_specs=pl.BlockSpec(memory_space=pltpu.VMEM),
        name="attend",
    )(place, queries, own, other, value_up)


def project(lifted, proj):
    return pl.pallas_call(
        project_kernel,
        out_shape=jax.ShapeDtypeStruct((N_X * N_Z, HALF, 128), jnp.bfloat16),
        in_specs=[pl.BlockSpec(memory_space=pltpu.VMEM)] * 2,
        out_specs=pl.BlockSpec(memory_space=pltpu.VMEM),
        name="project",
    )(lifted, proj)


def middle(place, shared):
    return pl.pallas_call(
        mid_kernel,
        out_shape=(
            jax.ShapeDtypeStruct((TOK, QUAD * 256), jnp.bfloat16),
            jax.ShapeDtypeStruct((TOK, 256), jnp.bfloat16),
        ),
        in_specs=[
            pl.BlockSpec(memory_space=pltpu.SMEM),
            pl.BlockSpec(memory_space=pltpu.VMEM),
        ],
        out_specs=(pl.BlockSpec(memory_space=pltpu.VMEM),) * 2,
        name="middle",
    )(place, shared)


def hidden(place, rows, weights):
    depth = D // QUAD
    return pl.pallas_call(
        hidden_kernel,
        out_shape=jax.ShapeDtypeStruct((QUAD, ROWS, QUAD * 128), jnp.bfloat16),
        grid=(QUAD,),
        in_specs=[
            pl.BlockSpec(memory_space=pltpu.SMEM),
            pl.BlockSpec(memory_space=pltpu.VMEM),
        ]
        + [pl.BlockSpec((depth, 256), lambda i: (i, 0))] * QUAD,
        out_specs=pl.BlockSpec((QUAD, ROWS, QUAD * 128), lambda i: (0, 0, 0)),
        scratch_shapes=[
            pltpu.VMEM((QUAD, ROWS, 256), jnp.float32),
            pltpu.VMEM((ROWS, 1), jnp.float32),
        ],
        name="hidden",
    )(place, rows, *weights)


def down(place, act, weights):
    return pl.pallas_call(
        down_kernel,
        out_shape=jax.ShapeDtypeStruct((ROWS, QUAD * 256), jnp.bfloat16),
        in_specs=[pl.BlockSpec(memory_space=pltpu.SMEM)]
        + [pl.BlockSpec(memory_space=pltpu.VMEM)] * (1 + QUAD),
        out_specs=pl.BlockSpec(memory_space=pltpu.VMEM),
        name="down",
    )(place, act, *weights)


def spread_over(x, axis, groups):
    count = len(groups[0])
    return lax.all_to_all(
        jnp.broadcast_to(x[None], (count,) + x.shape), axis, 0, 0, tiled=True, axis_index_groups=groups
    )


def quad_of(own, chip):
    core = lax.ppermute(own, "head", CORE_SWAP)
    return (own, core, chip, lax.ppermute(chip, "head", CORE_SWAP))


def per_device(
    tokens, queries, latents, value_up, out_proj, expert_ids, expert_gates, w_gate, w_up, w_down
):
    blk = lax.axis_index("blk")
    core = lax.axis_index("head") & 1

    moved = lax.ppermute(out_proj, ("blk", "head"), PROJ_MOVE)
    proj = lax.all_gather(moved, "blk", axis=0, tiled=True, axis_index_groups=Y_GROUPS)
    proj = proj.reshape(N_Y // 2, 2 * out_proj.shape[0], 128)

    half = lax.dynamic_slice(latents, (core * HALF, 0), (HALF, LAT + ROPE))
    column = spread_over(half, "blk", Y_GROUPS).reshape(N_Y * HALF, LAT + ROPE).T

    gate_up = jnp.concatenate([w_gate[0], w_up[0]], axis=1)
    gate_up_chip = lax.ppermute(gate_up, "head", CHIP_SWAP)
    down_chip = lax.ppermute(w_down[0], "head", CHIP_SWAP)
    gate_up_quad = quad_of(gate_up, gate_up_chip)
    down_quad = quad_of(w_down[0], down_chip)

    own = spread_over(column, "blk", X_GROUPS).reshape(N_X, LAT + ROPE, N_Y * HALF)
    other = lax.ppermute(own, "head", CORE_SWAP)

    place = jnp.stack([blk, core, lax.axis_index("head") & (QUAD - 1)]).astype(jnp.int32)
    lifted = attend(place, queries, own, other, value_up)

    lifted_row = lax.all_to_all(
        lifted, ("blk", "head"), 0, 0, tiled=True, axis_index_groups=XC_GROUPS
    )
    partial = project(lifted_row, proj)
    spread = lax.all_to_all(partial, ("blk", "head"), 0, 0, tiled=True, axis_index_groups=XZ_GROUPS)
    summed = jnp.sum(spread.reshape(N_X, N_Z, HALF, 128).astype(jnp.float32), axis=1)
    token_blocks = jnp.stack([tokens[:, :128], tokens[:, 128:]]).reshape(4, HALF, 128)
    shared = jnp.concatenate([summed, token_blocks.astype(jnp.float32)], axis=0)
    shared = spread_over(shared, "head", QUADS).reshape(QUAD, 8, HALF, 128)
    mid_quad, mid_state = middle(place, shared)
    mid_wide = mid_state.astype(jnp.float32)

    row_count = tokens.shape[0]
    flat_ids = expert_ids.reshape(-1)
    choose_count = expert_ids.shape[1]
    onehot_ids = (flat_ids[:, None] == jnp.arange(EXPERTS, dtype=jnp.int32)[None, :]).astype(
        jnp.int32
    )
    earlier = jnp.cumsum(onehot_ids, axis=0) - onehot_ids
    ranks = jnp.sum(earlier * onehot_ids, axis=1)
    slot_ids = flat_ids * CAP + ranks
    slot_hits = jnp.arange(SLOTS, dtype=jnp.int32)[:, None] == slot_ids[None, :]
    row_ids = jnp.arange(ROWS, dtype=jnp.int32)
    row_slots = row_ids // PART * CAP + place[2] * PART + row_ids % PART
    row_hits = row_slots[:, None] == slot_ids[None, :]
    select = jnp.sum(
        row_hits.astype(jnp.bfloat16).reshape(ROWS, row_count, choose_count), axis=2
    )
    combine = jnp.sum(
        jnp.where(slot_hits, expert_gates.reshape(-1)[None, :], 0.0).reshape(
            SLOTS, row_count, choose_count
        ),
        axis=2,
    )

    outgoing = (
        jnp.dot(select, mid_quad, preferred_element_type=jnp.float32)
        .astype(jnp.bfloat16)
        .reshape(N_BLK, PART * QUAD * 2, 128)
    )
    incoming = lax.all_to_all(outgoing, "blk", 0, 0, tiled=True)
    rows_here = incoming.reshape(ROWS, QUAD * 256)
    rows = spread_over(rows_here, "head", ACROSS).reshape(QUAD, ROWS, QUAD * 256)
    act = hidden(place, rows, gate_up_quad)
    acts = lax.all_to_all(act, "head", 0, 0, tiled=True, axis_index_groups=ACROSS)
    expert_out = down(place, acts, down_quad)
    sent = (
        expert_out.reshape(N_BLK, PART, QUAD, 256)
        .transpose(0, 2, 1, 3)
        .reshape(N_BLK * QUAD, PART * 2, 128)
    )
    returned = lax.all_to_all(
        sent, ("blk", "head"), 0, 0, tiled=True, axis_index_groups=BLK_QUAD
    )
    returned_wide = returned.reshape(SLOTS, 256).astype(jnp.float32)
    routed = jnp.einsum("sr,sd->rd", combine, returned_wide, precision=lax.Precision.HIGHEST)
    return (mid_wide + routed).astype(jnp.bfloat16)


def solution(mesh):
    placed = (
        P("blk", "head"),
        P("blk", "head"),
        P("blk", None),
        P("head", None, None),
        P("head", "blk"),
        P("blk", None),
        P("blk", None),
        P("blk", None, "head"),
        P("blk", None, "head"),
        P("blk", None, "head"),
    )

    return jax.shard_map(
        per_device, mesh=mesh, in_specs=placed, out_specs=P("blk", "head"), check_vma=False
    )
```

```python
import jax
import jax.numpy as jnp
from jax import lax
from jax.experimental import pallas as pl
from jax.experimental.pallas import tpu as pltpu
from jax.sharding import PartitionSpec as P


D = 4096
LAT = 512
ROPE = 64
QKNOPE = 128
VDIM = 128
EXPERTS = 32
CAP = 20
SLOTS = EXPERTS * CAP
TOK = 64
HALF = TOK // 2
N_BLK = 32
N_HEAD = 16
N_X = 4
N_Y = 8
HEADS_HERE = 4
SCALE = (QKNOPE + ROPE) ** (-0.5)

X_GROUPS = [[y * N_X + x for x in range(N_X)] for y in range(N_Y)]
Y_GROUPS = [[y * N_X + x for y in range(N_Y)] for x in range(N_X)]
N_Z = N_HEAD // 2


def device(y, x, z, core):
    return (y * N_X + x) * N_HEAD + z * 2 + core


XC_GROUPS = [
    [device(y, x, z, c) for x in range(N_X) for c in range(2)]
    for y in range(N_Y)
    for z in range(N_Z)
]
XZ_GROUPS = [
    [device(y, x, z, c) for x in range(N_X) for z in range(N_Z)]
    for y in range(N_Y)
    for c in range(2)
]
PROJ_MOVE = [
    (device(y, x, z, c), device((y & 6) | c, x, z, y & 1))
    for y in range(N_Y)
    for x in range(N_X)
    for z in range(N_Z)
    for c in range(2)
]
QUAD = 4
PART = CAP // QUAD
ROWS = N_BLK * PART
QUADS = [[q * QUAD + i for i in range(QUAD)] for q in range(N_HEAD // QUAD)]
ACROSS = [[q * QUAD + i for q in range(N_HEAD // QUAD)] for i in range(QUAD)]
BLK_QUAD = [
    [b * N_HEAD + q * QUAD + i for b in range(N_BLK) for i in range(QUAD)]
    for q in range(N_HEAD // QUAD)
]
CORE_SWAP = [(i, i ^ 1) for i in range(N_HEAD)]
CHIP_SWAP = [(i, i ^ 2) for i in range(N_HEAD)]


def attention_kernel(place_ref, q_ref, own_ref, other_ref, lift_ref, out_ref):
    width = LAT + ROPE
    q_all = q_ref[...]
    q_rows = jnp.concatenate(
        [q_all[:, h * width : (h + 1) * width] for h in range(HEADS_HERE)], axis=0
    )
    rows = HEADS_HERE * TOK
    first = place_ref[0] * TOK
    core = place_ref[1]
    query_pos = first + (lax.broadcasted_iota(jnp.int32, (rows, N_Y * HALF), 0) & (TOK - 1))
    key_idx = lax.broadcasted_iota(jnp.int32, (rows, N_Y * HALF), 1)
    room = query_pos - ((key_idx >> 5) * (N_X * TOK) + (key_idx & (HALF - 1)))
    chunks = [
        (ref, x, x * TOK + part * HALF)
        for part, ref in ((core, own_ref), (1 - core, other_ref))
        for x in range(N_X)
    ]
    scores = []
    row_max = None
    for ref, x, offset in chunks:
        raw = jnp.dot(q_rows, ref[x], preferred_element_type=jnp.float32)
        raw = jnp.where(room >= offset, raw * SCALE, -1e30)
        scores.append(raw)
        row_max = raw if row_max is None else jnp.maximum(row_max, raw)
    row_max = jnp.max(row_max, axis=1, keepdims=True)
    total = 0.0
    context = 0.0
    for (ref, x, offset), raw in zip(chunks, scores):
        weights = jnp.exp(raw - row_max)
        total = total + weights
        context = context + lax.dot_general(
            weights.astype(jnp.bfloat16),
            ref[x, :LAT],
            (((1,), (1,)), ((), ())),
            preferred_element_type=jnp.float32,
        )
    denominator = jnp.sum(total, axis=1, keepdims=True)
    context = (context / denominator).astype(jnp.bfloat16)
    for h in range(HEADS_HERE):
        lifted = jnp.dot(
            context[h * TOK : (h + 1) * TOK], lift_ref[h], preferred_element_type=jnp.float32
        ).astype(jnp.bfloat16)
        for member in range(2 * N_X):
            out_ref[member, :, h * VDIM : (h + 1) * VDIM] = lifted


def project_kernel(lifted_ref, proj_ref, out_ref):
    halves = [
        jnp.concatenate([lifted_ref[x * 2 + c] for x in range(N_X)], axis=0) for c in range(2)
    ]
    lifted = jnp.concatenate(halves, axis=1)
    for pair in range(N_Y // 4):
        weights = jnp.concatenate([proj_ref[2 * pair], proj_ref[2 * pair + 1]], axis=1)
        full = jnp.dot(lifted, weights, preferred_element_type=jnp.float32).astype(jnp.bfloat16)
        for side in range(2):
            for x in range(N_X):
                for p in range(2):
                    row = x * TOK + p * HALF
                    out_ref[x * N_Z + (2 * pair + side) * 2 + p] = full[
                        row : row + HALF, side * 128 : (side + 1) * 128
                    ]


def mid_kernel(place_ref, shared_ref, select_ref, out_ref, own_ref):
    for i in range(QUAD):
        parts = []
        for p in range(2):
            wide = [
                shared_ref[i, 4 + f * 2 + p] + shared_ref[p * 2 + i // 2, i % 2 * 2 + f]
                for f in range(2)
            ]
            parts.append(jnp.concatenate(wide, axis=1))
        mid = jnp.concatenate(parts, axis=0).astype(jnp.bfloat16)
        out_ref[:, i * 256 : (i + 1) * 256] = jnp.dot(
            select_ref[...], mid, preferred_element_type=jnp.float32
        ).astype(jnp.bfloat16)

        @pl.when(place_ref[2] == i)
        def _():
            own_ref[...] = mid


def hidden_kernel(place_ref, rows_ref, *refs):
    weight_refs, (out_ref, acc_ref, square_ref) = refs[:QUAD], refs[QUAD:]
    step = pl.program_id(0)

    @pl.when(step == 0)
    def _():
        acc_ref[...] = jnp.zeros_like(acc_ref)
        square_ref[...] = jnp.zeros_like(square_ref)

    rows = rows_ref[0]
    for j in range(QUAD):
        acc_ref[j] += jnp.dot(rows, weight_refs[j][...], preferred_element_type=jnp.float32)
    wide = rows.astype(jnp.float32)
    square_ref[...] += jnp.sum(wide * wide, axis=1, keepdims=True)

    @pl.when(step == QUAD - 1)
    def _():
        inverse = lax.rsqrt(square_ref[...] / D + 1e-06)
        for j in range(QUAD):
            owner = jnp.bitwise_xor(place_ref[2], j)
            gate = acc_ref[j, :, :128] * inverse
            up = acc_ref[j, :, 128:] * inverse
            act = (gate / (1.0 + jnp.exp(-gate)) * up).astype(jnp.bfloat16)
            for other in range(QUAD):

                @pl.when(owner == other)
                def _():
                    for q in range(QUAD):
                        out_ref[q, :, other * 128 : (other + 1) * 128] = act


def down_kernel(place_ref, act_ref, *refs):
    weight_refs, (out_ref, acc_ref) = refs[:QUAD], refs[QUAD:]
    step = pl.program_id(0)

    @pl.when(step == 0)
    def _():
        acc_ref[...] = jnp.zeros_like(acc_ref)

    act = act_ref[0]
    for j in range(QUAD):
        acc_ref[j] += jnp.dot(act, weight_refs[j][...], preferred_element_type=jnp.float32)

    @pl.when(step == QUAD - 1)
    def _():
        for j in range(QUAD):
            owner = jnp.bitwise_xor(place_ref[2], j)
            result = acc_ref[j].astype(jnp.bfloat16).astype(jnp.float32)
            for b in range(N_BLK):
                out_ref[b * QUAD + owner] = result[b * PART : (b + 1) * PART].astype(jnp.bfloat16)


def attend(place, queries, own, other, value_up):
    return pl.pallas_call(
        attention_kernel,
        out_shape=jax.ShapeDtypeStruct((2 * N_X, TOK, HEADS_HERE * VDIM), jnp.bfloat16),
        in_specs=[pl.BlockSpec(memory_space=pltpu.SMEM)]
        + [pl.BlockSpec(memory_space=pltpu.VMEM)] * 4,
        out_specs=pl.BlockSpec(memory_space=pltpu.VMEM),
        name="attend",
    )(place, queries, own, other, value_up)


def project(lifted, proj):
    return pl.pallas_call(
        project_kernel,
        out_shape=jax.ShapeDtypeStruct((N_X * N_Z, HALF, 128), jnp.bfloat16),
        in_specs=[pl.BlockSpec(memory_space=pltpu.VMEM)] * 2,
        out_specs=pl.BlockSpec(memory_space=pltpu.VMEM),
        name="project",
    )(lifted, proj)


def middle(place, shared, select):
    return pl.pallas_call(
        mid_kernel,
        out_shape=(
            jax.ShapeDtypeStruct((ROWS, QUAD * 256), jnp.bfloat16),
            jax.ShapeDtypeStruct((TOK, 256), jnp.bfloat16),
        ),
        in_specs=[pl.BlockSpec(memory_space=pltpu.SMEM)]
        + [pl.BlockSpec(memory_space=pltpu.VMEM)] * 2,
        out_specs=(pl.BlockSpec(memory_space=pltpu.VMEM),) * 2,
        name="middle",
    )(place, shared, select)


def hidden(place, rows, weights):
    depth = D // QUAD
    return pl.pallas_call(
        hidden_kernel,
        out_shape=jax.ShapeDtypeStruct((QUAD, ROWS, QUAD * 128), jnp.bfloat16),
        grid=(QUAD,),
        in_specs=[
            pl.BlockSpec(memory_space=pltpu.SMEM),
            pl.BlockSpec((1, ROWS, depth), lambda i: (i, 0, 0)),
        ]
        + [pl.BlockSpec((depth, 256), lambda i: (i, 0))] * QUAD,
        out_specs=pl.BlockSpec((QUAD, ROWS, QUAD * 128), lambda i: (0, 0, 0)),
        scratch_shapes=[
            pltpu.VMEM((QUAD, ROWS, 256), jnp.float32),
            pltpu.VMEM((ROWS, 1), jnp.float32),
        ],
        name="hidden",
    )(place, rows, *weights)


def down(place, act, weights):
    depth = QUAD * 128
    return pl.pallas_call(
        down_kernel,
        out_shape=jax.ShapeDtypeStruct((N_BLK * QUAD, PART, 256), jnp.bfloat16),
        grid=(QUAD,),
        in_specs=[
            pl.BlockSpec(memory_space=pltpu.SMEM),
            pl.BlockSpec((1, ROWS, depth), lambda i: (i, 0, 0)),
        ]
        + [pl.BlockSpec((depth, 256), lambda i: (i, 0))] * QUAD,
        out_specs=pl.BlockSpec((N_BLK * QUAD, PART, 256), lambda i: (0, 0, 0)),
        scratch_shapes=[pltpu.VMEM((QUAD, ROWS, 256), jnp.float32)],
        name="down",
    )(place, act, *weights)


def spread_over(x, axis, groups):
    count = len(groups[0])
    return lax.all_to_all(
        jnp.broadcast_to(x[None], (count,) + x.shape), axis, 0, 0, tiled=True, axis_index_groups=groups
    )


def quad_of(own, chip):
    core = lax.ppermute(own, "head", CORE_SWAP)
    return (own, core, chip, lax.ppermute(chip, "head", CORE_SWAP))


def per_device(
    tokens, queries, latents, value_up, out_proj, expert_ids, expert_gates, w_gate, w_up, w_down
):
    blk = lax.axis_index("blk")
    core = lax.axis_index("head") & 1

    moved = lax.ppermute(out_proj, ("blk", "head"), PROJ_MOVE)
    proj = lax.all_gather(moved, "blk", axis=0, tiled=True, axis_index_groups=Y_GROUPS)
    proj = proj.reshape(N_Y // 2, 2 * out_proj.shape[0], 128)

    half = lax.dynamic_slice(latents, (core * HALF, 0), (HALF, LAT + ROPE))
    column = spread_over(half, "blk", Y_GROUPS).reshape(N_Y * HALF, LAT + ROPE).T

    gate_up = jnp.concatenate([w_gate[0], w_up[0]], axis=1)
    gate_up_chip = lax.ppermute(gate_up, "head", CHIP_SWAP)
    down_chip = lax.ppermute(w_down[0], "head", CHIP_SWAP)
    gate_up_quad = quad_of(gate_up, gate_up_chip)
    down_quad = quad_of(w_down[0], down_chip)

    own = spread_over(column, "blk", X_GROUPS).reshape(N_X, LAT + ROPE, N_Y * HALF)
    other = lax.ppermute(own, "head", CORE_SWAP)

    place = jnp.stack([blk, core, lax.axis_index("head") & (QUAD - 1)]).astype(jnp.int32)
    lifted = attend(place, queries, own, other, value_up)

    lifted_row = lax.all_to_all(
        lifted, ("blk", "head"), 0, 0, tiled=True, axis_index_groups=XC_GROUPS
    )
    partial = project(lifted_row, proj)
    spread = lax.all_to_all(partial, ("blk", "head"), 0, 0, tiled=True, axis_index_groups=XZ_GROUPS)
    summed = jnp.sum(spread.reshape(N_X, N_Z, HALF, 128).astype(jnp.float32), axis=1)
    token_blocks = jnp.stack([tokens[:, :128], tokens[:, 128:]]).reshape(4, HALF, 128)
    shared = jnp.concatenate([summed, token_blocks.astype(jnp.float32)], axis=0)
    shared = spread_over(shared, "head", QUADS).reshape(QUAD, 8, HALF, 128)
    row_count = tokens.shape[0]
    flat_ids = expert_ids.reshape(-1)
    choose_count = expert_ids.shape[1]
    onehot_ids = (flat_ids[:, None] == jnp.arange(EXPERTS, dtype=jnp.int32)[None, :]).astype(
        jnp.int32
    )
    earlier = jnp.cumsum(onehot_ids, axis=0) - onehot_ids
    ranks = jnp.sum(earlier * onehot_ids, axis=1)
    slot_ids = flat_ids * CAP + ranks
    slot_hits = jnp.arange(SLOTS, dtype=jnp.int32)[:, None] == slot_ids[None, :]
    row_ids = jnp.arange(ROWS, dtype=jnp.int32)
    row_slots = row_ids // PART * CAP + place[2] * PART + row_ids % PART
    row_hits = row_slots[:, None] == slot_ids[None, :]
    select = jnp.sum(
        row_hits.astype(jnp.bfloat16).reshape(ROWS, row_count, choose_count), axis=2
    )
    combine = jnp.sum(
        jnp.where(slot_hits, expert_gates.reshape(-1)[None, :], 0.0).reshape(
            SLOTS, row_count, choose_count
        ),
        axis=2,
    )

    chosen, mid_state = middle(place, shared, select)
    mid_wide = mid_state.astype(jnp.float32)
    outgoing = chosen.reshape(N_BLK, PART * QUAD * 2, 128)
    incoming = lax.all_to_all(outgoing, "blk", 0, 0, tiled=True)
    rows_here = incoming.reshape(ROWS, QUAD * 256)
    rows = spread_over(rows_here, "head", ACROSS).reshape(QUAD, ROWS, QUAD * 256)
    act = hidden(place, rows, gate_up_quad)
    acts = lax.all_to_all(act, "head", 0, 0, tiled=True, axis_index_groups=ACROSS)
    sent = down(place, acts, down_quad)
    returned = lax.all_to_all(
        sent, ("blk", "head"), 0, 0, tiled=True, axis_index_groups=BLK_QUAD
    )
    returned_wide = returned.reshape(SLOTS, 256).astype(jnp.float32)
    routed = jnp.einsum("sr,sd->rd", combine, returned_wide, precision=lax.Precision.HIGHEST)
    return (mid_wide + routed).astype(jnp.bfloat16)


def solution(mesh):
    placed = (
        P("blk", "head"),
        P("blk", "head"),
        P("blk", None),
        P("head", None, None),
        P("head", "blk"),
        P("blk", None),
        P("blk", None),
        P("blk", None, "head"),
        P("blk", None, "head"),
        P("blk", None, "head"),
    )

    return jax.shard_map(
        per_device, mesh=mesh, in_specs=placed, out_specs=P("blk", "head"), check_vma=False
    )
```
